32 devices in a mesh: groups: 2 (over y), seq: 8 (over z, x), tp: 2 (over core).
Axes of the slice: x: 2, y: 2, z: 4, core: 2. Of those that a mesh axis runs over, the one named last changes fastest.
Arguments:
- span_queries: bfloat16 [128, 64, 128], P(('groups', 'seq'), 'tp'), parts along dimension 0, may hold values from -180 to 180
- span_keys: bfloat16 [128, 4, 128], P(('groups', 'seq'), 'tp'), parts along dimension 0, may hold values from -9 to 9
- span_values: bfloat16 [128, 4, 128], P(('groups', 'seq'), 'tp'), parts along dimension 0, may hold values from -6.5 to 6.5
- prefix_keys: bfloat16 [1152, 4, 128], P(('groups', 'seq'), 'tp'), parts along dimension 0, may hold values from -9 to 9
- prefix_values: bfloat16 [1152, 4, 128], P(('groups', 'seq'), 'tp'), parts along dimension 0, may hold values from -6.5 to 6.5
- prefix_lengths: int32 [16], P('groups'), parts along dimension 0, may hold values from 1 to 72
- decode_queries: bfloat16 [32, 64, 128], P(('groups', 'seq'), 'tp'), parts along dimension 0, may hold values from -180 to 180
- decode_new_keys: bfloat16 [32, 4, 128], P(('groups', 'seq'), 'tp'), parts along dimension 0, may hold values from -6 to 6
- decode_new_values: bfloat16 [32, 4, 128], P(('groups', 'seq'), 'tp'), parts along dimension 0, may hold values from -6 to 6
- decode_key_cache: bfloat16 [64, 256, 4, 128], P(('groups', 'seq'), None, 'tp'), parts along dimension 0, may hold values from -6 to 6
- decode_value_cache: bfloat16 [64, 256, 4, 128], P(('groups', 'seq'), None, 'tp'), parts along dimension 0, may hold values from -6 to 6
- owner_map: int32 [32, 1], P('groups'), parts along dimension 0, may hold values from 0 to 7; in each aligned block of 16 rows (0 to 15, 16 to 31, ...) at most 4 rows name the same one
- decode_lengths: int32 [32], P('groups'), parts along dimension 0, may hold values from 1 to 256
Outputs:
- prefill_out: bfloat16 [128, 64, 128], P(('groups', 'seq'), 'tp'), parts along dimension 0
- decode_out: bfloat16 [64, 64, 128], P(('groups', 'seq'), 'tp'), parts along dimension 0
The draws below stay inside these ranges and needn't reach their ends.
There are 2 independent parts, one for each index of `groups`. The reference program is written for one: setup_inputs(seed, part) draws one part's arguments, and reference() takes and returns one part's arrays. A program takes and returns all parts, laid end to end along the dimension named above; each array names one. Nothing has to cross between parts.
Inputs may be any that keep to these rules, and one draw needn't show every extreme that they name: `owner_map`: no shard owns more than 4 requests, and some shard owns exactly 4.
All inputs are finite; a program needn't handle non-finite values.
Results may differ from the reference program's by a relative error of at most 0.005.
Values may be sent and summed in bfloat16 or wider, within the bound.
A program may use at most 64 MiB of HBM per device.

```python
import math
import jax
import jax.numpy as jnp
import numpy as np
from jax import lax

H = 64
KVH = 4
HD = 128
CH_DEV = 8
PRE_DEV = 72
CTX = 256
SLOTS = 4
SPAN = 64
PREFIX = 576
REQS = 16
OWN = 32
N_SEQ = 8


def noisy_queries(key, rows):
    base = jax.random.truncated_normal(key, -4.0, 4.0, (rows, H, HD), jnp.float32) * 1.7
    return base.astype(jnp.bfloat16)


def shard_scales(key, blocks, marker, lower, upper):
    scale_key = jax.random.fold_in(key, marker)
    return jnp.exp(jax.random.uniform(scale_key, (blocks, 1, KVH, 1), jnp.float32, jnp.log(lower), jnp.log(upper)))


def scale_range():
    lower, upper = (0.3, 1.7)
    return (lower, upper)


def scaled_keys(key, rows, width, marker):
    blocks = rows // width
    lower, upper = scale_range()
    scales = shard_scales(key, blocks, marker, lower, upper)
    entries = jax.random.truncated_normal(jax.random.fold_in(key, marker + 1), -4.0, 4.0, (blocks, width, KVH, HD), jnp.float32)
    factor = jnp.exp(jax.random.uniform(jax.random.fold_in(key, marker + 2), (blocks, width, KVH, 1), jnp.float32, jnp.log(0.8), jnp.log(1.25)))
    return (entries * scales * factor).reshape(rows, KVH, HD).astype(jnp.bfloat16)


def offset_values(key, rows, width, marker):
    blocks = rows // width
    entries = jax.random.truncated_normal(jax.random.fold_in(key, marker + 3), -4.0, 4.0, (blocks, width, KVH, HD), jnp.float32)
    return entries.reshape(rows, KVH, HD).astype(jnp.bfloat16)


def draw_span_queries(key, part):
    return noisy_queries(jax.random.fold_in(key, 11), SPAN)


def draw_decode_queries(key, part):
    return noisy_queries(jax.random.fold_in(key, 13), REQS)


def draw_prefix_keys(key, part):
    return scaled_keys(key, PREFIX, PRE_DEV, 201)


def draw_prefix_values(key, part):
    return offset_values(key, PREFIX, PRE_DEV, 201)


def draw_span_keys(key, part):
    return scaled_keys(key, SPAN, CH_DEV, 301)


def draw_span_values(key, part):
    return offset_values(key, SPAN, CH_DEV, 301)


def set_ends(drawn, rng, least, high):
    longest = drawn.shape.index(max(drawn.shape))
    spots = []
    for shift in (0, 1):
        where = [jax.random.randint(jax.random.fold_in(rng, axis), (), 0, length) for axis, length in enumerate(drawn.shape)]
        where[longest] = (where[longest] + shift) % drawn.shape[longest]
        spots.append(tuple(where))
    return drawn.at[spots[0]].set(least).at[spots[1]].set(high)


def steps_of(own_key, shape, pieces, low, top_value):
    def one(axis_at, parts):
        heights = jax.random.uniform(jax.random.fold_in(jax.random.fold_in(own_key, 6), axis_at), (parts,), jnp.float32, low / len(pieces), top_value / len(pieces))
        return jnp.repeat(jnp.exp(heights), shape[axis_at] // parts).reshape((-1,) + (1,) * (len(shape) - axis_at - 1))

    loudness = one(*pieces[0])
    for cut in pieces[1:]:
        loudness = loudness * one(*cut)
    return loudness


def assign_block(key, own, number, rows, amount, top, bound, skew):
    order = jax.random.permutation(key, amount)
    packed, usual = shares(amount, rows * top, bound, skew, True), shares(amount, rows * top, bound, skew, False)
    places = jnp.arange(amount)

    def named(sizes, rotation):
        used = int((sizes > 0).sum())
        fixed = max(1, used // 4)
        passed = fixed + (places - fixed + rotation * (used - fixed)) % max(1, amount - fixed)
        return jnp.zeros((amount,), jnp.int32).at[order[jnp.where(places < fixed, places, passed)]].set(jnp.asarray(sizes, jnp.int32))

    sizes = jnp.where(number % 4 == 0, named(packed, number // 4), named(usual, number - number // 4 - 1))
    mixed = jax.random.permutation(jax.random.fold_in(own, 3), amount)
    giver, sink = mixed[0:amount // 2 * 2:2], mixed[1:amount // 2 * 2:2]
    margin = jnp.minimum(sizes[giver] - 1, bound - sizes[sink]) // 2
    margin = jnp.where((giver == order[0]) | (sink == order[0]) | (sizes[sink] == 0), 0, jnp.maximum(margin, 0))
    passed = jax.random.randint(jax.random.fold_in(own, 4), (amount // 2,), 0, 1 << 20) % (margin + 1)
    sizes = sizes.at[giver].add(-passed).at[sink].add(passed)
    items = jnp.searchsorted(jnp.cumsum(sizes), jnp.arange(rows * top), side="right").astype(jnp.int32)
    grid = items.reshape(top, rows).T
    grid = grid[jax.random.permutation(jax.random.fold_in(own, 1), rows)]
    rotation = jax.random.randint(jax.random.fold_in(own, 2), (rows, 1), 0, top)
    return jnp.take_along_axis(grid, (jnp.arange(top)[None, :] + rotation) % top, axis=1)


def shares(count, total, limit, slope, full):
    portions = [(1 << 20) // math.isqrt(grade ** slope) + 1 for grade in range(1, count + 1)]
    largest = limit if full else min(limit, max(-(-total // count), total * portions[0] // sum(portions)))
    least = 1 if total - largest >= count - 1 else 0
    holding, surplus = [largest] + [least] * (count - 1), total - largest - least * (count - 1)
    while surplus > 0:
        free = [i for i in range(1, count) if holding[i] < largest] or [i for i in range(1, count) if holding[i] < limit]
        pool, remaining = sum([portions[i] for i in free]), surplus
        for i in free:
            addition = min(limit - holding[i], max(1, remaining * portions[i] // pool), surplus)
            holding[i] = holding[i] + addition
            surplus = surplus - addition
    return np.array(holding)


def normal_values(key, shape, deviation, bound, cuts=(), kind=jnp.bfloat16):
    array = deviation * jax.random.normal(key, shape, jnp.float32)
    if cuts:
        array = array * steps_of(key, shape, cuts, -0.22, 0.18)
    return jnp.clip(array, -bound, bound).astype(kind)


def setup_inputs(seed: int = 0, part: int = 0) -> dict:
    key_of = jax.random.split(jax.random.key(seed), 14)
    part_splits = jax.random.split(jax.random.fold_in(key_of[13], part), 14)
    span_queries = draw_span_queries(jax.random.fold_in(jax.random.fold_in(key_of[13], part), 71), part)
    span_keys = draw_span_keys(jax.random.fold_in(jax.random.fold_in(key_of[13], part), 71), part)
    span_values = draw_span_values(jax.random.fold_in(jax.random.fold_in(key_of[13], part), 71), part)
    prefix_keys = draw_prefix_keys(jax.random.fold_in(jax.random.fold_in(key_of[13], part), 71), part)
    prefix_values = draw_prefix_values(jax.random.fold_in(jax.random.fold_in(key_of[13], part), 71), part)
    prefix_lengths = set_ends(jax.random.randint(part_splits[5], (N_SEQ,), 1, PRE_DEV + 1), jax.random.fold_in(part_splits[5], 1), 1, PRE_DEV).astype(jnp.int32)
    decode_queries = draw_decode_queries(jax.random.fold_in(jax.random.fold_in(key_of[13], part), 71), part)
    decode_new_keys = normal_values(part_splits[7], (REQS, KVH, HD), 1.7, 6.0, ((0, 8), (1, 2)))
    decode_new_values = normal_values(part_splits[8], (REQS, KVH, HD), 1.0, 6.0, ((0, 8), (1, 2)))
    decode_key_cache = normal_values(part_splits[9], (OWN, CTX, KVH, HD), 1.7, 6.0, ((0, 8), (2, 2)))
    decode_value_cache = normal_values(part_splits[10], (OWN, CTX, KVH, HD), 1.0, 6.0, ((0, 8), (2, 2)))
    owner_map_keys = jax.random.split(jax.random.fold_in(part_splits[11], 1), REQS // REQS)
    owner_map_turns = jax.random.permutation(jax.random.fold_in(part_splits[11], 3), REQS // REQS)
    owner_map = jax.vmap(lambda own, number: assign_block(jax.random.fold_in(part_splits[11], 2), own, number, REQS, N_SEQ, 1, SLOTS, 2))(owner_map_keys, owner_map_turns).reshape((REQS, 1))
    decode_lengths = set_ends(jax.random.randint(part_splits[12], (REQS,), 1, CTX + 1), jax.random.fold_in(part_splits[12], 1), 1, CTX).astype(jnp.int32)
    return dict(span_queries=span_queries, span_keys=span_keys, span_values=span_values, prefix_keys=prefix_keys, prefix_values=prefix_values, prefix_lengths=prefix_lengths, decode_queries=decode_queries, decode_new_keys=decode_new_keys, decode_new_values=decode_new_values, decode_key_cache=decode_key_cache, decode_value_cache=decode_value_cache, owner_map=owner_map, decode_lengths=decode_lengths)


def attend(queries, key_rows, value_rows, allowed):
    tokens = queries.shape[0]
    grouped = queries.reshape(tokens, KVH, H // KVH, HD).astype(jnp.float32)
    scores = jnp.einsum("tkgd,skd->tkgs", grouped, key_rows.astype(jnp.float32)) * (HD ** -0.5)
    visible = allowed[:, None, None, :]
    scores = jnp.where(visible, scores, -1.0e30)
    running_max = jnp.max(scores, axis=-1, keepdims=True)
    weights = jnp.where(visible, jnp.exp(scores - running_max), 0.0)
    normalizer = jnp.sum(weights, axis=-1)
    rounded = lax.optimization_barrier(weights.astype(jnp.bfloat16)).astype(jnp.float32)
    mixed = jnp.einsum("tkgs,skd->tkgd", rounded, value_rows.astype(jnp.float32))
    return (mixed / normalizer[..., None]).reshape(tokens, H, HD).astype(jnp.bfloat16)


def reference(span_queries, span_keys, span_values, prefix_keys, prefix_values, prefix_lengths, decode_queries, decode_new_keys, decode_new_values, decode_key_cache, decode_value_cache, owner_map, decode_lengths):
    position = jnp.arange(PREFIX, dtype=jnp.int32)
    prefix_live = (position % PRE_DEV) < prefix_lengths[position // PRE_DEV]
    all_keys = jnp.concatenate([prefix_keys, span_keys], axis=0)
    all_values = jnp.concatenate([prefix_values, span_values], axis=0)
    span_position = jnp.arange(SPAN, dtype=jnp.int32)

    def one_block(block_index):
        queries = lax.dynamic_slice_in_dim(span_queries, block_index * CH_DEV, CH_DEV)
        token_index = block_index * CH_DEV + jnp.arange(CH_DEV, dtype=jnp.int32)
        causal = span_position[None, :] <= token_index[:, None]
        allowed = jnp.concatenate([jnp.broadcast_to(prefix_live[None, :], (CH_DEV, PREFIX)), causal], axis=1)
        return attend(queries, all_keys, all_values, allowed)

    blocks = lax.map(one_block, jnp.arange(N_SEQ, dtype=jnp.int32))
    prefill_out = blocks.reshape(SPAN, H, HD)

    owners = owner_map[:, 0]
    order = jnp.arange(REQS, dtype=jnp.int32)
    earlier = (owners[None, :] == owners[:, None]) & (order[None, :] < order[:, None])
    ranking = jnp.sum(earlier.astype(jnp.int32), axis=1)
    slot_index = (owners * SLOTS + ranking).astype(jnp.int32)
    context_index = jnp.arange(CTX, dtype=jnp.int32)

    def one_request(items):
        query, new_key, new_value, length, slot = items
        cached_keys = lax.dynamic_index_in_dim(decode_key_cache, slot, 0, keepdims=False)
        cached_values = lax.dynamic_index_in_dim(decode_value_cache, slot, 0, keepdims=False)
        key_rows = jnp.concatenate([cached_keys, new_key[None]], axis=0)
        value_rows = jnp.concatenate([cached_values, new_value[None]], axis=0)
        allowed = jnp.concatenate([context_index < length, jnp.ones((1,), dtype=bool)])
        return attend(query[None], key_rows, value_rows, allowed[None])[0]

    outputs = lax.map(one_request, (decode_queries, decode_new_keys, decode_new_values, decode_lengths, slot_index))
    decode_out = jnp.zeros((OWN, H, HD), jnp.bfloat16).at[slot_index].set(outputs)
    return prefill_out, decode_out
```

```python
import functools
import math

import jax
import jax.numpy as jnp
from jax import lax
from jax.experimental import pallas as pl
from jax.experimental.pallas import tpu as pltpu
from jax.sharding import PartitionSpec as P

LOWEST = -1e30
MESH = pl.DeviceIdType.MESH
NT = (((1,), (1,)), ((), ()))
TN = (((0,), (0,)), ((), ()))
NN = (((1,), (0,)), ((), ()))
KEYS, VALUES, QUERIES, NEW = range(4)


def repeat(low, high, body, carry, unrolled):
    if unrolled:
        for step in range(low, high):
            carry = body(step, carry)
        return carry
    return lax.fori_loop(low, high, body, carry)


def kernel(
    n,
    tokens,
    heads,
    kv,
    span_q,
    span_k,
    span_v,
    prefix_k,
    prefix_v,
    prefix_len,
    dec_q,
    new_k,
    new_v,
    cache_k,
    cache_v,
    owner,
    dec_len,
    out_prefill,
    out_decode,
    q_buf,
    k_buf,
    v_buf,
    dq_buf,
    new_buf,
    ck_buf,
    cv_buf,
    plen,
    own,
    dlen,
    local_sem,
    send_sem,
    recv_sem,
):
    me = lax.axis_index("seq")
    group = heads // kv
    prefix_rows = prefix_k.shape[0]
    span_rows = span_k.shape[0]
    here = dec_q.shape[0]
    requests = own.shape[0]
    slots = cache_k.shape[0]
    factor = q_buf.shape[-1] ** (-0.5) * math.log2(math.e)
    half = (n + 1) // 2
    small = n <= 16

    odd = me % 2
    place = (1 - odd) * (me // 2) + odd * (n - 1 - me // 2)

    def index_at(spot):
        spot = lax.rem(spot + 2 * n, n)
        upper = (spot >= half).astype(jnp.int32) if not isinstance(spot, int) else int(spot >= half)
        return (1 - upper) * (2 * spot) + upper * (2 * (n - 1 - spot) + 1)

    right, left = index_at(place + 1), index_at(place - 1)

    locals_ = [
        pltpu.make_async_copy(source, target, local_sem.at[at])
        for at, (source, target) in enumerate(
            (
                (dec_q, dq_buf.at[pl.ds(me * here, here)]),
                (new_k, new_buf.at[me, 0]),
                (new_v, new_buf.at[me, 1]),
                (prefix_k, k_buf.at[me, pl.ds(0, prefix_rows)]),
                (span_k, k_buf.at[me, pl.ds(prefix_rows, span_rows)]),
                (prefix_v, v_buf.at[me, pl.ds(0, prefix_rows)]),
                (span_v, v_buf.at[me, pl.ds(prefix_rows, span_rows)]),
                (span_q, q_buf),
                (prefix_len, plen),
                (owner, own),
                (dec_len, dlen),
                (cache_k, ck_buf),
                (cache_v, cv_buf),
            )
        )
    ]
    barrier = pltpu.get_barrier_semaphore()
    for neighbour in (left, right):
        pl.semaphore_signal(barrier, inc=1, device_id={"seq": neighbour}, device_id_type=MESH)
    for copy in locals_:
        copy.start()
    pl.semaphore_wait(barrier, 2)

    def part(kind, index):
        if kind == KEYS:
            return k_buf.at[index]
        if kind == VALUES:
            return v_buf.at[index]
        if kind == QUERIES:
            return dq_buf.at[pl.ds(index * here, here)]
        return new_buf.at[index]

    def message(way, step, kind, arriving=False):
        sign = 1 if way == 0 else -1
        index = index_at(place - sign * (step + (1 if arriving else 0)))
        return pltpu.make_async_remote_copy(
            src_ref=part(kind, index),
            dst_ref=part(kind, index),
            send_sem=send_sem.at[way, step, kind],
            recv_sem=recv_sem.at[way, step, kind],
            device_id={"seq": right if way == 0 else left},
            device_id_type=MESH,
        )

    full = (n - 1) // 2
    split = n % 2 == 0
    kinds_of_split = ((QUERIES, KEYS), (NEW, VALUES))
    order = (QUERIES, NEW, KEYS, VALUES)

    def send(step, kinds):
        for kind in kinds:
            for way in (0, 1):
                message(way, step, kind).start()

    def send_last(kinds):
        for way in (0, 1):
            for kind in kinds_of_split[way]:
                if kind in kinds:
                    message(way, full, kind).start()

    def dispatch(step, kinds):
        if full == 0:
            send_last(kinds)
        else:
            send(step, kinds)

    locals_[0].wait()
    dispatch(0, (QUERIES,))
    locals_[1].wait()
    locals_[2].wait()
    dispatch(0, (NEW,))
    locals_[3].wait()
    locals_[4].wait()
    dispatch(0, (KEYS,))
    locals_[5].wait()
    locals_[6].wait()
    dispatch(0, (VALUES,))
    locals_[7].wait()
    locals_[8].wait()

    rows = prefix_rows + span_rows
    lanes = q_buf.shape[0]
    row = lax.broadcasted_iota(jnp.int32, (rows, lanes), 0)
    lane = lax.broadcasted_iota(jnp.int32, (rows, lanes), 1)
    match = (row % kv) == (lane % heads) // group
    query_time = jnp.where(match, me * tokens + lane // heads, -1)
    in_prefix = row < prefix_rows
    span_time = (row - prefix_rows) // kv

    def attend(shard, carry):
        top, total, mixed = carry
        scores = lax.dot_general(
            k_buf[shard], q_buf[...], NT, preferred_element_type=jnp.float32
        )
        key_time = jnp.where(
            in_prefix,
            jnp.where(row < plen[shard] * kv, 0, n * tokens),
            span_time + shard * tokens,
        )
        scores = jnp.where(key_time <= query_time, scores, LOWEST)
        new_top = jnp.maximum(top, jnp.max(scores, axis=0, keepdims=True))
        weights = jnp.exp2((scores - new_top) * factor)
        decay = jnp.exp2((top - new_top) * factor)
        total = total * decay + jnp.sum(weights, axis=0, keepdims=True)
        mixed = mixed * decay + lax.dot_general(
            v_buf[shard], weights.astype(jnp.bfloat16), TN, preferred_element_type=jnp.float32
        )
        return new_top, total, mixed

    carry = (
        jnp.full((1, lanes), LOWEST, jnp.float32),
        jnp.zeros((1, lanes), jnp.float32),
        jnp.zeros((q_buf.shape[1], lanes), jnp.float32),
    )
    carry = attend(me, carry)

    def arrive(step, kinds, forward):
        for kind in kinds:
            for way in (0, 1):
                message(way, step, kind, True).wait_recv()
                if forward == "full":
                    message(way, step + 1, kind).start()
                elif forward == "split" and kind in kinds_of_split[way]:
                    message(way, full, kind).start()

    def ring_step(step, carry):
        arrive(step, order, "full")
        carry = attend(index_at(place - step - 1), carry)
        return attend(index_at(place + step + 1), carry)

    carry = repeat(0, full - 1, ring_step, carry, small)
    if full >= 1:
        arrive(full - 1, order, "split" if split else None)
        carry = attend(index_at(place - full), carry)
        carry = attend(index_at(place + full), carry)
    if split:
        message(0, full, QUERIES, True).wait_recv()
        message(1, full, NEW, True).wait_recv()

    for copy in locals_[9:]:
        copy.wait()

    def find(request, found):
        count, picks = found
        mine = own[request] == me
        picks = tuple(
            jnp.where(mine & (count == slot), request, pick) for slot, pick in enumerate(picks)
        )
        return count + jnp.where(mine, 1, 0), picks

    count, picks = repeat(
        0, requests, find, (jnp.int32(0), tuple(jnp.int32(0) for _ in range(slots))), small
    )
    cols = ck_buf.shape[1]
    head = lax.broadcasted_iota(jnp.int32, (heads, cols), 0)
    col = lax.broadcasted_iota(jnp.int32, (heads, cols), 1)
    bound = jnp.where(col % kv == head // group, col, cols)

    def spread(pair):
        pair = pair.astype(jnp.float32)
        return jnp.concatenate(
            [jnp.broadcast_to(pair[j : j + 1], (group, pair.shape[1])) for j in range(kv)], axis=0
        )

    for slot in range(slots):
        pick = picks[slot]
        queries = dq_buf[pick]
        own_key = spread(new_buf[pick // here, 0, pick % here])
        own_value = spread(new_buf[pick // here, 1, pick % here])
        scores = lax.dot_general(queries, ck_buf[slot], NT, preferred_element_type=jnp.float32)
        scores = jnp.where(bound < dlen[pick] * kv, scores, LOWEST)
        own_score = jnp.sum(queries.astype(jnp.float32) * own_key, axis=1, keepdims=True)
        top = jnp.maximum(jnp.max(scores, axis=1, keepdims=True), own_score)
        weights = jnp.exp2((scores - top) * factor)
        own_weight = jnp.exp2((own_score - top) * factor)
        total = jnp.sum(weights, axis=1, keepdims=True) + own_weight
        mixed = lax.dot_general(
            weights.astype(jnp.bfloat16), cv_buf[slot], NN, preferred_element_type=jnp.float32
        )
        mixed = mixed + own_weight.astype(jnp.bfloat16).astype(jnp.float32) * own_value
        result = jnp.where(slot < count, mixed / total, 0.0)
        out_decode[slot] = result.astype(out_decode.dtype)

    if split:
        message(0, full, KEYS, True).wait_recv()
        message(1, full, VALUES, True).wait_recv()
        carry = attend(index_at(place + full + 1), carry)
    top, total, mixed = carry
    out_prefill[...] = (mixed / total).T.astype(out_prefill.dtype)

    def finish(step, unused):
        for kind in order:
            for way in (0, 1):
                message(way, step, kind).wait_send()
        return unused

    repeat(0, full, finish, 0, small)
    if split:
        for way in (0, 1):
            for kind in kinds_of_split[way]:
                message(way, full, kind).wait_send()


def on_device(
    n,
    span_queries,
    span_keys,
    span_values,
    prefix_keys,
    prefix_values,
    prefix_lengths,
    decode_queries,
    decode_new_keys,
    decode_new_values,
    decode_key_cache,
    decode_value_cache,
    owner_map,
    decode_lengths,
):
    tokens, heads, dim = span_queries.shape
    kv = span_keys.shape[1]
    slots, context = decode_key_cache.shape[:2]
    here = decode_queries.shape[0]
    requests = owner_map.shape[0]
    rows = (prefix_keys.shape[0] + tokens) * kv
    steps = max(1, n // 2)
    bf16 = jnp.bfloat16
    any_space = pl.BlockSpec(memory_space=pl.ANY)
    vmem = pl.BlockSpec(memory_space=pltpu.VMEM)
    prefill, decode = pl.pallas_call(
        functools.partial(kernel, n, tokens, heads, kv),
        out_shape=(
            jax.ShapeDtypeStruct((tokens * heads, dim), bf16),
            jax.ShapeDtypeStruct((slots, heads, dim), bf16),
        ),
        in_specs=[any_space] * 13,
        out_specs=(vmem, vmem),
        scratch_shapes=[
            pltpu.VMEM((tokens * heads, dim), bf16),
            pltpu.VMEM((n, rows, dim), bf16),
            pltpu.VMEM((n, rows, dim), bf16),
            pltpu.VMEM((requests, heads, dim), bf16),
            pltpu.VMEM((n, 2, here, kv, dim), bf16),
            pltpu.VMEM((slots, context * kv, dim), bf16),
            pltpu.VMEM((slots, context * kv, dim), bf16),
            pltpu.SMEM(prefix_lengths.shape, jnp.int32),
            pltpu.SMEM((requests,), jnp.int32),
            pltpu.SMEM(decode_lengths.shape, jnp.int32),
            pltpu.SemaphoreType.DMA((13,)),
            pltpu.SemaphoreType.DMA((2, steps, 4)),
            pltpu.SemaphoreType.DMA((2, steps, 4)),
        ],
        compiler_params=pltpu.CompilerParams(collective_id=0, has_side_effects=True),
        name="mixed_attention",
    )(
        span_queries.reshape(tokens * heads, dim),
        span_keys.reshape(tokens * kv, dim),
        span_values.reshape(tokens * kv, dim),
        prefix_keys.reshape(-1, dim),
        prefix_values.reshape(-1, dim),
        prefix_lengths,
        decode_queries,
        decode_new_keys,
        decode_new_values,
        decode_key_cache.reshape(slots, context * kv, dim),
        decode_value_cache.reshape(slots, context * kv, dim),
        owner_map.reshape(requests),
        decode_lengths,
    )
    return prefill.reshape(tokens, heads, dim), decode


def solution(mesh):
    rows = P(("groups", "seq"), "tp", None)
    cache = P(("groups", "seq"), None, "tp", None)
    return jax.shard_map(
        functools.partial(on_device, mesh.shape["seq"]),
        mesh=mesh,
        in_specs=(
            rows,
            rows,
            rows,
            rows,
            rows,
            P("groups"),
            rows,
            rows,
            rows,
            cache,
            cache,
            P("groups", None),
            P("groups"),
        ),
        out_specs=(rows, rows),
        check_vma=False,
    )
```

```python
import functools
import math

import jax
import jax.numpy as jnp
from jax import lax
from jax.experimental import pallas as pl
from jax.experimental.pallas import tpu as pltpu
from jax.sharding import PartitionSpec as P

LOWEST = -1e30
MESH = pl.DeviceIdType.MESH
NT = (((1,), (1,)), ((), ()))
TN = (((0,), (0,)), ((), ()))
NN = (((1,), (0,)), ((), ()))
KEYS, VALUES, QUERIES, NEW = range(4)


def repeat(low, high, body, carry, unrolled):
    if unrolled:
        for step in range(low, high):
            carry = body(step, carry)
        return carry
    return lax.fori_loop(low, high, body, carry)


def kernel(
    n,
    tokens,
    heads,
    kv,
    span_q,
    span_k,
    span_v,
    prefix_k,
    prefix_v,
    prefix_len,
    dec_q,
    new_k,
    new_v,
    cache_k,
    cache_v,
    owner,
    dec_len,
    out_prefill,
    out_decode,
    q_buf,
    k_buf,
    v_buf,
    dq_buf,
    new_buf,
    ck_buf,
    cv_buf,
    plen,
    own,
    dlen,
    local_sem,
    send_sem,
    recv_sem,
):
    me = lax.axis_index("seq")
    group = heads // kv
    prefix_rows = prefix_k.shape[0]
    span_rows = span_k.shape[0]
    here = dec_q.shape[0]
    requests = own.shape[0]
    slots = cache_k.shape[0]
    factor = q_buf.shape[-1] ** (-0.5) * math.log2(math.e)
    half = (n + 1) // 2
    small = n <= 16

    odd = me % 2
    place = (1 - odd) * (me // 2) + odd * (n - 1 - me // 2)

    def index_at(spot):
        spot = lax.rem(spot + 2 * n, n)
        upper = (spot >= half).astype(jnp.int32) if not isinstance(spot, int) else int(spot >= half)
        return (1 - upper) * (2 * spot) + upper * (2 * (n - 1 - spot) + 1)

    right, left = index_at(place + 1), index_at(place - 1)

    locals_ = [
        pltpu.make_async_copy(source, target, local_sem.at[at])
        for at, (source, target) in enumerate(
            (
                (dec_q, dq_buf.at[pl.ds(me * here, here)]),
                (new_k, new_buf.at[me, 0]),
                (new_v, new_buf.at[me, 1]),
                (prefix_k, k_buf.at[me, pl.ds(0, prefix_rows)]),
                (span_k, k_buf.at[me, pl.ds(prefix_rows, span_rows)]),
                (prefix_v, v_buf.at[me, pl.ds(0, prefix_rows)]),
                (span_v, v_buf.at[me, pl.ds(prefix_rows, span_rows)]),
                (span_q, q_buf),
                (prefix_len, plen),
                (owner, own),
                (dec_len, dlen),
                (cache_k, ck_buf),
                (cache_v, cv_buf),
            )
        )
    ]
    barrier = pltpu.get_barrier_semaphore()
    for neighbour in (left, right):
        pl.semaphore_signal(barrier, inc=1, device_id={"seq": neighbour}, device_id_type=MESH)
    for copy in locals_:
        copy.start()
    pl.semaphore_wait(barrier, 2)

    def part(kind, index):
        if kind == KEYS:
            return k_buf.at[index]
        if kind == VALUES:
            return v_buf.at[index]
        if kind == QUERIES:
            return dq_buf.at[pl.ds(index * here, here)]
        return new_buf.at[index]

    def message(way, step, kind, arriving=False):
        sign = 1 if way == 0 else -1
        index = index_at(place - sign * (step + (1 if arriving else 0)))
        return pltpu.make_async_remote_copy(
            src_ref=part(kind, index),
            dst_ref=part(kind, index),
            send_sem=send_sem.at[way, step, kind],
            recv_sem=recv_sem.at[way, step, kind],
            device_id={"seq": right if way == 0 else left},
            device_id_type=MESH,
        )

    full = (n - 1) // 2
    split = n % 2 == 0
    kinds_of_split = ((QUERIES, KEYS), (NEW, VALUES))
    order = (QUERIES, NEW, KEYS, VALUES)

    def send(step, kinds):
        for kind in kinds:
            for way in (0, 1):
                message(way, step, kind).start()

    def send_last(kinds):
        for way in (0, 1):
            for kind in kinds_of_split[way]:
                if kind in kinds:
                    message(way, full, kind).start()

    def dispatch(step, kinds):
        if full == 0:
            send_last(kinds)
        else:
            send(step, kinds)

    locals_[0].wait()
    dispatch(0, (QUERIES,))
    locals_[1].wait()
    locals_[2].wait()
    dispatch(0, (NEW,))
    locals_[3].wait()
    locals_[4].wait()
    dispatch(0, (KEYS,))
    locals_[5].wait()
    locals_[6].wait()
    dispatch(0, (VALUES,))
    locals_[7].wait()
    locals_[8].wait()

    rows = prefix_rows + span_rows
    lanes = q_buf.shape[0]
    row = lax.broadcasted_iota(jnp.int32, (rows, lanes), 0)
    lane = lax.broadcasted_iota(jnp.int32, (rows, lanes), 1)
    match = (row % kv) == (lane % heads) // group
    query_time = jnp.where(match, me * tokens + lane // heads, -1)
    in_prefix = row < prefix_rows
    span_time = (row - prefix_rows) // kv

    def attend(shard, carry):
        top, total, mixed = carry
        scores = lax.dot_general(
            k_buf[shard], q_buf[...], NT, preferred_element_type=jnp.float32
        )
        key_time = jnp.where(
            in_prefix,
            jnp.where(row < plen[shard] * kv, 0, n * tokens),
            span_time + shard * tokens,
        )
        scores = jnp.where(key_time <= query_time, scores, LOWEST)
        new_top = jnp.maximum(top, jnp.max(scores, axis=0, keepdims=True))
        weights = jnp.exp2((scores - new_top) * factor)
        decay = jnp.exp2((top - new_top) * factor)
        total = total * decay + jnp.sum(weights, axis=0, keepdims=True)
        mixed = mixed * decay + lax.dot_general(
            v_buf[shard], weights.astype(jnp.bfloat16), TN, preferred_element_type=jnp.float32
        )
        return new_top, total, mixed

    carry = (
        jnp.full((1, lanes), LOWEST, jnp.float32),
        jnp.zeros((1, lanes), jnp.float32),
        jnp.zeros((q_buf.shape[1], lanes), jnp.float32),
    )
    carry = attend(me, carry)

    def arrive(step, kinds, forward):
        for kind in kinds:
            for way in (0, 1):
                message(way, step, kind, True).wait_recv()
                if forward == "full":
                    message(way, step + 1, kind).start()
                elif forward == "split" and kind in kinds_of_split[way]:
                    message(way, full, kind).start()

    def ring_step(step, carry):
        arrive(step, order, "full")
        carry = attend(index_at(place - step - 1), carry)
        return attend(index_at(place + step + 1), carry)

    carry = repeat(0, full - 1, ring_step, carry, small)
    if full >= 1:
        arrive(full - 1, order, "split" if split else None)
        carry = attend(index_at(place - full), carry)
        carry = attend(index_at(place + full), carry)
    if split:
        message(0, full, QUERIES, True).wait_recv()
        message(1, full, NEW, True).wait_recv()

    for copy in locals_[9:]:
        copy.wait()

    def find(request, found):
        count, picks = found
        mine = own[request] == me
        picks = tuple(
            jnp.where(mine & (count == slot), request, pick) for slot, pick in enumerate(picks)
        )
        return count + jnp.where(mine, 1, 0), picks

    count, picks = repeat(
        0, requests, find, (jnp.int32(0), tuple(jnp.int32(0) for _ in range(slots))), small
    )
    cols = ck_buf.shape[1]
    head = lax.broadcasted_iota(jnp.int32, (heads, cols), 0)
    col = lax.broadcasted_iota(jnp.int32, (heads, cols), 1)
    bound = jnp.where(col % kv == head // group, col, cols)

    def spread(pair):
        pair = pair.astype(jnp.float32)
        return jnp.concatenate(
            [jnp.broadcast_to(pair[j : j + 1], (group, pair.shape[1])) for j in range(kv)], axis=0
        )

    for slot in range(slots):
        pick = picks[slot]
        queries = dq_buf[pick]
        own_key = spread(new_buf[pick // here, 0, pick % here])
        own_value = spread(new_buf[pick // here, 1, pick % here])
        scores = lax.dot_general(queries, ck_buf[slot], NT, preferred_element_type=jnp.float32)
        scores = jnp.where(bound < dlen[pick] * kv, scores, LOWEST)
        own_score = jnp.sum(queries.astype(jnp.float32) * own_key, axis=1, keepdims=True)
        top = jnp.maximum(jnp.max(scores, axis=1, keepdims=True), own_score)
        weights = jnp.exp2((scores - top) * factor)
        own_weight = jnp.exp2((own_score - top) * factor)
        total = jnp.sum(weights, axis=1, keepdims=True) + own_weight
        mixed = lax.dot_general(
            weights.astype(jnp.bfloat16), cv_buf[slot], NN, preferred_element_type=jnp.float32
        )
        mixed = mixed + own_weight.astype(jnp.bfloat16).astype(jnp.float32) * own_value
        result = jnp.where(slot < count, mixed / total, 0.0)
        out_decode[slot] = result.astype(out_decode.dtype)

    if split:
        message(0, full, KEYS, True).wait_recv()
        message(1, full, VALUES, True).wait_recv()
        carry = attend(index_at(place + full + 1), carry)
    top, total, mixed = carry
    out_prefill[...] = (mixed / total).T.astype(out_prefill.dtype)

    def finish(step, unused):
        for kind in order:
            for way in (0, 1):
                message(way, step, kind).wait_send()
        return unused

    repeat(0, full, finish, 0, small)
    if split:
        for way in (0, 1):
            for kind in kinds_of_split[way]:
                message(way, full, kind).wait_send()


def on_device(
    n,
    span_queries,
    span_keys,
    span_values,
    prefix_keys,
    prefix_values,
    prefix_lengths,
    decode_queries,
    decode_new_keys,
    decode_new_values,
    decode_key_cache,
    decode_value_cache,
    owner_map,
    decode_lengths,
):
    tokens, heads, dim = span_queries.shape
    kv = span_keys.shape[1]
    slots, context = decode_key_cache.shape[:2]
    here = decode_queries.shape[0]
    requests = owner_map.shape[0]
    rows = (prefix_keys.shape[0] + tokens) * kv
    steps = max(1, n // 2)
    bf16 = jnp.bfloat16
    any_space = pl.BlockSpec(memory_space=pl.ANY)
    vmem = pl.BlockSpec(memory_space=pltpu.VMEM)
    prefill, decode = pl.pallas_call(
        functools.partial(kernel, n, tokens, heads, kv),
        out_shape=(
            pltpu.VMEM((tokens * heads, dim), bf16),
            pltpu.VMEM((slots, heads, dim), bf16),
        ),
        in_specs=[any_space] * 13,
        out_specs=(vmem, vmem),
        scratch_shapes=[
            pltpu.VMEM((tokens * heads, dim), bf16),
            pltpu.VMEM((n, rows, dim), bf16),
            pltpu.VMEM((n, rows, dim), bf16),
            pltpu.VMEM((requests, heads, dim), bf16),
            pltpu.VMEM((n, 2, here, kv, dim), bf16),
            pltpu.VMEM((slots, context * kv, dim), bf16),
            pltpu.VMEM((slots, context * kv, dim), bf16),
            pltpu.SMEM(prefix_lengths.shape, jnp.int32),
            pltpu.SMEM((requests,), jnp.int32),
            pltpu.SMEM(decode_lengths.shape, jnp.int32),
            pltpu.SemaphoreType.DMA((13,)),
            pltpu.SemaphoreType.DMA((2, steps, 4)),
            pltpu.SemaphoreType.DMA((2, steps, 4)),
        ],
        compiler_params=pltpu.CompilerParams(collective_id=0, has_side_effects=True),
        name="mixed_attention",
    )(
        span_queries.reshape(tokens * heads, dim),
        span_keys.reshape(tokens * kv, dim),
        span_values.reshape(tokens * kv, dim),
        prefix_keys.reshape(-1, dim),
        prefix_values.reshape(-1, dim),
        prefix_lengths,
        decode_queries,
        decode_new_keys,
        decode_new_values,
        decode_key_cache.reshape(slots, context * kv, dim),
        decode_value_cache.reshape(slots, context * kv, dim),
        owner_map.reshape(requests),
        decode_lengths,
    )
    return prefill.reshape(tokens, heads, dim), decode


def solution(mesh):
    rows = P(("groups", "seq"), "tp", None)
    cache = P(("groups", "seq"), None, "tp", None)
    return jax.shard_map(
        functools.partial(on_device, mesh.shape["seq"]),
        mesh=mesh,
        in_specs=(
            rows,
            rows,
            rows,
            rows,
            rows,
            P("groups"),
            rows,
            rows,
            rows,
            cache,
            cache,
            P("groups", None),
            P("groups"),
        ),
        out_specs=(rows, rows),
        check_vma=False,
    )
```

```python
import functools
import math

import jax
import jax.numpy as jnp
from jax import lax
from jax.experimental import pallas as pl
from jax.experimental.pallas import tpu as pltpu
from jax.sharding import PartitionSpec as P

LOWEST = -1e30
MESH = pl.DeviceIdType.MESH
NT = (((1,), (1,)), ((), ()))
TN = (((0,), (0,)), ((), ()))
NN = (((1,), (0,)), ((), ()))
KEYS, VALUES, QUERIES, NEW = range(4)
ACROSS, ALONG, RELAY = range(3)


def repeat(low, high, body, carry, unrolled):
    if unrolled:
        for step in range(low, high):
            carry = body(step, carry)
        return carry
    return lax.fori_loop(low, high, body, carry)


def kernel(
    n,
    tokens,
    heads,
    kv,
    span_q,
    span_k,
    span_v,
    prefix_k,
    prefix_v,
    prefix_len,
    dec_q,
    new_k,
    new_v,
    cache_k,
    cache_v,
    owner,
    dec_len,
    out_prefill,
    out_decode,
    q_buf,
    k_buf,
    v_buf,
    dq_buf,
    new_buf,
    ck_buf,
    cv_buf,
    plen,
    own,
    dlen,
    local_sem,
    send_sem,
    recv_sem,
):
    me = lax.axis_index("seq")
    group = heads // kv
    prefix_rows = prefix_k.shape[0]
    span_rows = span_k.shape[0]
    here = dec_q.shape[0]
    requests = own.shape[0]
    slots = cache_k.shape[0]
    factor = q_buf.shape[-1] ** (-0.5) * math.log2(math.e)
    half = (n + 1) // 2
    small = n <= 16

    depth = n // 2
    chip, column = me // 2, me % 2
    partner = 2 * chip + 1 - column
    paired = depth & (depth - 1) == 0
    relayed = depth == 4
    inner = (chip % 3 + 1) // 2 if relayed else 0

    def hop(turn, back=False):
        if not paired:
            return 2 * lax.rem(chip + (depth - turn if back else turn), depth) + column
        spot = 0
        for bit in range(depth.bit_length() - 1):
            own_bit, turn_bit = (chip // 2**bit) % 2, (turn // 2**bit) % 2
            spot = spot + 2**bit * (own_bit + turn_bit - 2 * own_bit * turn_bit)
        return 2 * spot + column

    locals_ = [
        pltpu.make_async_copy(source, target, local_sem.at[at])
        for at, (source, target) in enumerate(
            (
                (dec_q, dq_buf.at[pl.ds(me * here, here)]),
                (new_k, new_buf.at[me, 0]),
                (new_v, new_buf.at[me, 1]),
                (prefix_k, k_buf.at[me, pl.ds(0, prefix_rows)]),
                (span_k, k_buf.at[me, pl.ds(prefix_rows, span_rows)]),
                (prefix_v, v_buf.at[me, pl.ds(0, prefix_rows)]),
                (span_v, v_buf.at[me, pl.ds(prefix_rows, span_rows)]),
                (span_q, q_buf),
                (prefix_len, plen),
                (owner, own),
                (dec_len, dlen),
                (cache_k, ck_buf),
                (cache_v, cv_buf),
            )
        )
    ]
    barrier = pltpu.get_barrier_semaphore()

    def hello(target):
        pl.semaphore_signal(barrier, inc=1, device_id={"seq": target}, device_id_type=MESH)

    def greet(turn, unused):
        if relayed and turn == 3:
            pl.when(inner == 1)(lambda: hello(hop(turn)))
        else:
            hello(hop(turn))
        return unused

    hello(partner)
    repeat(1, depth, greet, 0, small)
    for copy in locals_:
        copy.start()
    pl.semaphore_wait(barrier, depth - 1 + inner if relayed else depth)

    def part(kind, index):
        if kind == KEYS:
            return k_buf.at[index]
        if kind == VALUES:
            return v_buf.at[index]
        if kind == QUERIES:
            return dq_buf.at[pl.ds(index * here, here)]
        return new_buf.at[index]

    def message(role, turn, kind, index, target):
        return pltpu.make_async_remote_copy(
            src_ref=part(kind, index),
            dst_ref=part(kind, index),
            send_sem=send_sem.at[role, turn, kind],
            recv_sem=recv_sem.at[index, kind],
            device_id={"seq": target},
            device_id_type=MESH,
        )

    def arrived(kind, index):
        message(ACROSS, 0, kind, index, partner).wait_recv()

    order = (QUERIES, NEW, KEYS, VALUES)

    def along(turn, kind, action):
        copy = message(ALONG, turn, kind, me, hop(turn))
        if relayed and turn == 3:
            pl.when(inner == 1)(lambda: action(copy))
        else:
            action(copy)

    def relay(turn, kind, action):
        if relayed:
            copy = message(RELAY, 0, kind, hop(2), hop(1))
            pl.when((inner == 1) & (turn == 2))(lambda: action(copy))

    def start(copy):
        copy.start()

    def finish_send(copy):
        copy.wait_send()

    def dispatch(kind):
        message(ACROSS, 0, kind, me, partner).start()

        def go(turn, unused):
            along(turn, kind, start)
            return unused

        if relayed:
            for turn in (2, 3, 1):
                go(turn, 0)
        else:
            repeat(1, depth, go, 0, small)

    locals_[0].wait()
    dispatch(QUERIES)
    locals_[1].wait()
    locals_[2].wait()
    dispatch(NEW)
    locals_[3].wait()
    locals_[4].wait()
    dispatch(KEYS)
    locals_[5].wait()
    locals_[6].wait()
    dispatch(VALUES)
    locals_[7].wait()
    locals_[8].wait()

    rows = prefix_rows + span_rows
    lanes = q_buf.shape[0]
    row = lax.broadcasted_iota(jnp.int32, (rows, lanes), 0)
    lane = lax.broadcasted_iota(jnp.int32, (rows, lanes), 1)
    match = (row % kv) == (lane % heads) // group
    query_time = jnp.where(match, me * tokens + lane // heads, -1)
    in_prefix = row < prefix_rows
    span_time = (row - prefix_rows) // kv

    def attend(shard, carry):
        top, total, mixed = carry
        scores = lax.dot_general(
            k_buf[shard], q_buf[...], NT, preferred_element_type=jnp.float32
        )
        key_time = jnp.where(
            in_prefix,
            jnp.where(row < plen[shard] * kv, 0, n * tokens),
            span_time + shard * tokens,
        )
        scores = jnp.where(key_time <= query_time, scores, LOWEST)
        new_top = jnp.maximum(top, jnp.max(scores, axis=0, keepdims=True))
        weights = jnp.exp2((scores - new_top) * factor)
        decay = jnp.exp2((top - new_top) * factor)
        total = total * decay + jnp.sum(weights, axis=0, keepdims=True)
        mixed = mixed * decay + lax.dot_general(
            v_buf[shard], weights.astype(jnp.bfloat16), TN, preferred_element_type=jnp.float32
        )
        return new_top, total, mixed

    carry = (
        jnp.full((1, lanes), LOWEST, jnp.float32),
        jnp.zeros((1, lanes), jnp.float32),
        jnp.zeros((q_buf.shape[1], lanes), jnp.float32),
    )
    carry = attend(me, carry)

    def turn_at(step):
        if not relayed:
            return step + 1
        return (1 + inner, 2 + inner, 3 - 2 * inner)[step]

    def pass_on(step, kind):
        turn = turn_at(step)
        source = hop(turn, True)
        arrived(kind, source)
        relay(turn, kind, start)
        message(ACROSS, turn, kind, source, partner).start()
        return source

    def pass_all(kind):
        def go(step, unused):
            pass_on(step, kind)
            return unused

        repeat(0, depth - 1, go, 0, small)

    pass_all(QUERIES)
    pass_all(NEW)
    pass_all(KEYS)
    arrived(KEYS, partner)
    arrived(VALUES, partner)
    carry = attend(partner, carry)

    def take(step, carry):
        return attend(pass_on(step, VALUES), carry)

    carry = repeat(0, depth - 1, take, carry, small)

    def other(source):
        return source + 1 - 2 * column

    arrived(QUERIES, partner)
    arrived(NEW, partner)

    def settle(step, unused):
        arrived(QUERIES, other(hop(turn_at(step), True)))
        arrived(NEW, other(hop(turn_at(step), True)))
        return unused

    repeat(0, depth - 1, settle, 0, small)
    for copy in locals_[9:]:
        copy.wait()

    def find(request, found):
        count, picks = found
        mine = own[request] == me
        picks = tuple(
            jnp.where(mine & (count == slot), request, pick) for slot, pick in enumerate(picks)
        )
        return count + jnp.where(mine, 1, 0), picks

    count, picks = repeat(
        0, requests, find, (jnp.int32(0), tuple(jnp.int32(0) for _ in range(slots))), small
    )
    cols = ck_buf.shape[1]
    head = lax.broadcasted_iota(jnp.int32, (heads, cols), 0)
    col = lax.broadcasted_iota(jnp.int32, (heads, cols), 1)
    bound = jnp.where(col % kv == head // group, col, cols)

    def spread(pair):
        pair = pair.astype(jnp.float32)
        return jnp.concatenate(
            [jnp.broadcast_to(pair[j : j + 1], (group, pair.shape[1])) for j in range(kv)], axis=0
        )

    for slot in range(slots):
        pick = picks[slot]
        queries = dq_buf[pick]
        own_key = spread(new_buf[pick // here, 0, pick % here])
        own_value = spread(new_buf[pick // here, 1, pick % here])
        scores = lax.dot_general(queries, ck_buf[slot], NT, preferred_element_type=jnp.float32)
        scores = jnp.where(bound < dlen[pick] * kv, scores, LOWEST)
        own_score = jnp.sum(queries.astype(jnp.float32) * own_key, axis=1, keepdims=True)
        top = jnp.maximum(jnp.max(scores, axis=1, keepdims=True), own_score)
        weights = jnp.exp2((scores - top) * factor)
        own_weight = jnp.exp2((own_score - top) * factor)
        total = jnp.sum(weights, axis=1, keepdims=True) + own_weight
        mixed = lax.dot_general(
            weights.astype(jnp.bfloat16), cv_buf[slot], NN, preferred_element_type=jnp.float32
        )
        mixed = mixed + own_weight.astype(jnp.bfloat16).astype(jnp.float32) * own_value
        result = jnp.where(slot < count, mixed / total, 0.0)
        out_decode[slot] = result.astype(out_decode.dtype)

    def close(step, carry):
        source = other(hop(turn_at(step), True))
        arrived(KEYS, source)
        arrived(VALUES, source)
        return attend(source, carry)

    carry = repeat(0, depth - 1, close, carry, small)
    top, total, mixed = carry
    out_prefill[...] = (mixed / total).T.astype(out_prefill.dtype)

    for kind in order:
        message(ACROSS, 0, kind, me, partner).wait_send()
        relay(2, kind, finish_send)

        def finish(turn, unused):
            along(turn, kind, finish_send)
            message(ACROSS, turn, kind, hop(turn, True), partner).wait_send()
            return unused

        repeat(1, depth, finish, 0, small)


def store(prefill, decode, out_prefill, out_decode, sem):
    copies = (
        pltpu.make_async_copy(prefill, out_prefill, sem.at[0]),
        pltpu.make_async_copy(decode, out_decode, sem.at[1]),
    )
    for copy in copies:
        copy.start()
    for copy in copies:
        copy.wait()


def on_device(
    n,
    span_queries,
    span_keys,
    span_values,
    prefix_keys,
    prefix_values,
    prefix_lengths,
    decode_queries,
    decode_new_keys,
    decode_new_values,
    decode_key_cache,
    decode_value_cache,
    owner_map,
    decode_lengths,
):
    tokens, heads, dim = span_queries.shape
    kv = span_keys.shape[1]
    slots, context = decode_key_cache.shape[:2]
    here = decode_queries.shape[0]
    requests = owner_map.shape[0]
    rows = (prefix_keys.shape[0] + tokens) * kv
    bf16 = jnp.bfloat16
    any_space = pl.BlockSpec(memory_space=pl.ANY)
    vmem = pl.BlockSpec(memory_space=pltpu.VMEM)
    prefill, decode = pl.pallas_call(
        functools.partial(kernel, n, tokens, heads, kv),
        out_shape=(
            pltpu.VMEM((tokens * heads, dim), bf16),
            pltpu.VMEM((slots, heads, dim), bf16),
        ),
        in_specs=[any_space] * 13,
        out_specs=(vmem, vmem),
        scratch_shapes=[
            pltpu.VMEM((tokens * heads, dim), bf16),
            pltpu.VMEM((n, rows, dim), bf16),
            pltpu.VMEM((n, rows, dim), bf16),
            pltpu.VMEM((requests, heads, dim), bf16),
            pltpu.VMEM((n, 2, here, kv, dim), bf16),
            pltpu.VMEM((slots, context * kv, dim), bf16),
            pltpu.VMEM((slots, context * kv, dim), bf16),
            pltpu.SMEM(prefix_lengths.shape, jnp.int32),
            pltpu.SMEM((requests,), jnp.int32),
            pltpu.SMEM(decode_lengths.shape, jnp.int32),
            pltpu.SemaphoreType.DMA((13,)),
            pltpu.SemaphoreType.DMA((3, n // 2, 4)),
            pltpu.SemaphoreType.DMA((n, 4)),
        ],
        compiler_params=pltpu.CompilerParams(collective_id=0, has_side_effects=True),
        name="mixed_attention",
    )(
        span_queries.reshape(tokens * heads, dim),
        span_keys.reshape(tokens * kv, dim),
        span_values.reshape(tokens * kv, dim),
        prefix_keys.reshape(-1, dim),
        prefix_values.reshape(-1, dim),
        prefix_lengths,
        decode_queries,
        decode_new_keys,
        decode_new_values,
        decode_key_cache.reshape(slots, context * kv, dim),
        decode_value_cache.reshape(slots, context * kv, dim),
        owner_map.reshape(requests),
        decode_lengths,
    )
    prefill, decode = pl.pallas_call(
        store,
        out_shape=(
            jax.ShapeDtypeStruct((tokens * heads, dim), bf16),
            jax.ShapeDtypeStruct((slots, heads, dim), bf16),
        ),
        in_specs=[vmem, vmem],
        out_specs=[any_space, any_space],
        scratch_shapes=[pltpu.SemaphoreType.DMA((2,))],
        name="store_outputs",
    )(*(pltpu.with_memory_space_constraint(x, pltpu.VMEM) for x in (prefill, decode)))
    return prefill.reshape(tokens, heads, dim), decode


def solution(mesh):
    rows = P(("groups", "seq"), "tp", None)
    cache = P(("groups", "seq"), None, "tp", None)
    return jax.shard_map(
        functools.partial(on_device, mesh.shape["seq"]),
        mesh=mesh,
        in_specs=(
            rows,
            rows,
            rows,
            rows,
            rows,
            P("groups"),
            rows,
            rows,
            rows,
            cache,
            cache,
            P("groups", None),
            P("groups"),
        ),
        out_specs=(rows, rows),
        check_vma=False,
    )
```
